256 devices in a mesh: seq: 64 (over z, y, core), chan: 4 (over x).
Axes of the slice: x: 4, y: 4, z: 8, core: 2. Of those that a mesh axis runs over, the one named last changes fastest.
Arguments:
- signal: bfloat16 [16384, 2048], P('seq', 'chan'), may hold values from -6 to 6
- gate_rows: bfloat16 [16384, 2048], P('seq', 'chan'), may hold values from -60 to 60
- skip_gain: float32 [2048], P('chan'), may hold values from 0.5 to 1.5
- filter_taps: bfloat16 [16384, 16], P(None, 'chan'), may hold values from -2 to 2
- queries: bfloat16 [16384, 2048], P('seq', 'chan'), may hold values from -6 to 6
- key_rows: bfloat16 [16384, 2048], P('seq', 'chan'), may hold values from -6 to 6
Outputs:
- conv_mixed: bfloat16 [16384, 2048], P('seq', 'chan')
- attended: bfloat16 [256, 1024, 128], P(('chan', 'seq'))
The draws below stay inside these ranges and needn't reach their ends.
All inputs are finite; a program needn't handle non-finite values.
Results may differ from the reference program's by a relative error of at most 0.0061.
Values may be sent and summed in bfloat16 or wider, within the bound.
A program may use at most 128 MiB of HBM per device.

```python
import math
import jax
import jax.numpy as jnp
from jax import lax

HALF_HEADS = 16
HD = 128
DW = 2048
SEQUENCE_LENGTH = 16384
QB = 16
QROWS = 16
QLEN = 1024
N_SEQ = 64


def draw_queries(key, part):
    base = jax.random.fold_in(key, 1)
    drawn = jnp.clip(jax.random.normal(base, (SEQUENCE_LENGTH, DW), jnp.float32), -4.0, 4.0)
    return drawn.astype(jnp.bfloat16)


def draw_key_rows(key, part):
    base = jax.random.fold_in(key, 2)
    drawn = jnp.clip(jax.random.normal(base, (SEQUENCE_LENGTH, DW), jnp.float32), -4.0, 4.0)
    return drawn.astype(jnp.bfloat16)


def draw_gate_rows(key, part):
    base = jax.random.fold_in(key, 4)
    key_collection = jax.random.split(base, 3)
    ramp = jnp.exp(math.log(10.0) * jnp.arange(DW, dtype=jnp.float32) / max(DW - 1, 1)) / math.sqrt(10.0)
    columns = ramp * jax.random.uniform(key_collection[1], (DW,), jnp.float32, 0.7, 1.4)
    row_scale = jnp.exp(jax.random.uniform(key_collection[2], (SEQUENCE_LENGTH, 1), jnp.float32, 0.0, math.log(10.0))) / math.sqrt(10.0)
    drawn = jnp.clip(jax.random.normal(key_collection[0], (SEQUENCE_LENGTH, DW), jnp.float32), -4.0, 4.0)
    return (drawn * row_scale * columns[None, :]).astype(jnp.bfloat16)


def draw_filter_taps(key, part):
    base = jax.random.fold_in(key, 5)
    key_collection = jax.random.split(base, 6)
    slow_share = 0.6
    slow_heads = jax.random.uniform(key_collection[0], (HALF_HEADS,), jnp.float32) < slow_share
    tau_slow = jnp.exp(jax.random.uniform(key_collection[1], (HALF_HEADS,), jnp.float32, math.log(SEQUENCE_LENGTH / 2.0), math.log(8.0 * SEQUENCE_LENGTH)))
    tau_fast = jnp.exp(jax.random.uniform(key_collection[2], (HALF_HEADS,), jnp.float32, math.log(20.0), math.log(60.0)))
    decay_len = jnp.where(slow_heads, tau_slow, tau_fast)
    delay_index = jnp.arange(SEQUENCE_LENGTH, dtype=jnp.float32)[:, None]
    spike_positions = jax.random.randint(key_collection[3], (4, HALF_HEADS), 0, SEQUENCE_LENGTH).astype(jnp.float32)
    spike_keep_mask = jax.random.uniform(key_collection[4], (4, HALF_HEADS), jnp.float32, 0.5, 0.8)
    spike_values = jnp.prod(jnp.where(delay_index[None, :, :] >= spike_positions[:, None, :], spike_keep_mask[:, None, :], 1.0), axis=0)
    decay_ratio = jnp.exp(-2.0 / decay_len)
    energy = (1.0 - decay_ratio ** SEQUENCE_LENGTH) / (1.0 - decay_ratio)
    decay_profile = jnp.exp(-delay_index / decay_len[None, :]) / jnp.sqrt(energy)[None, :]
    noisy_filter_taps = jnp.clip(jax.random.normal(key_collection[5], (SEQUENCE_LENGTH, HALF_HEADS), jnp.float32), -4.0, 4.0)
    return (noisy_filter_taps * decay_profile * spike_values).astype(jnp.bfloat16)


def steps_of(rng, dims, cuts, low, high):
    gain, own = 1.0, jax.random.fold_in(rng, 6)
    for dim, blocks in cuts:
        steps = jnp.exp(jax.random.uniform(jax.random.fold_in(own, dim), (blocks,), jnp.float32, low / len(cuts), high / len(cuts)))
        gain = gain * jnp.repeat(steps, dims[dim] // blocks).reshape([-1 if axis == dim else 1 for axis in range(len(dims))])
    return gain


def gaussian(stream_key, shape, width, reach, pieces=(), kind=jnp.bfloat16):
    values = jax.random.normal(stream_key, shape, jnp.float32) * width
    if len(pieces) > 0:
        values = steps_of(stream_key, shape, pieces, -0.22, 0.18) * values
    return jnp.clip(values, min=-reach, max=reach).astype(kind)


def setup_inputs(seed: int = 0) -> dict:
    seeds = jax.random.split(jax.random.key(seed), 7)
    return {
        "signal": gaussian(seeds[0], (SEQUENCE_LENGTH, DW), 1.0, 6.0, ((0, 64), (1, 4))),
        "gate_rows": draw_gate_rows(jax.random.fold_in(seeds[6], 71), 0),
        "skip_gain": jnp.clip(0.5 + 1.0 * jax.random.uniform(seeds[2], (DW,), jnp.float32) ** steps_of(seeds[2], (DW,), ((0, 4),), -0.2, 0.2), 0.5, 1.5),
        "filter_taps": draw_filter_taps(jax.random.fold_in(seeds[6], 71), 0),
        "queries": draw_queries(jax.random.fold_in(seeds[6], 71), 0),
        "key_rows": draw_key_rows(jax.random.fold_in(seeds[6], 71), 0),
    }


def reference(signal, gate_rows, skip_gain, filter_taps, queries, key_rows):
    length = SEQUENCE_LENGTH
    inputs = signal.astype(jnp.float32)
    channel_taps = jnp.repeat(filter_taps.astype(jnp.float32), HD, axis=1)
    spectrum = jnp.fft.rfft(inputs, 2 * length, axis=0) * jnp.fft.rfft(channel_taps, 2 * length, axis=0)
    conv_sum = jnp.fft.irfft(spectrum, 2 * length, axis=0)[:length].astype(jnp.float32)
    conv_mixed = (gate_rows.astype(jnp.float32) * (conv_sum + skip_gain[None, :] * inputs)).astype(jnp.bfloat16)
    widened = conv_mixed.astype(jnp.float32)
    inv_scale = lax.rsqrt(lax.optimization_barrier(jnp.sum(widened * widened, axis=1)) / DW + 1e-06)
    values = (widened * inv_scale[:, None]).astype(jnp.bfloat16)
    head_q = queries.reshape(length, HALF_HEADS, HD).transpose(1, 0, 2)
    head_k = key_rows.reshape(length, HALF_HEADS, HD).transpose(1, 0, 2)
    head_v = values.reshape(length, HALF_HEADS, HD).transpose(1, 0, 2)
    block_len = min(1024, length)
    score_scale = 1.0 / math.sqrt(HD)

    def one_head(operands):
        q_head, k_head, v_head = operands
        q_blocks = q_head.reshape(length // block_len, block_len, HD)
        firsts = jnp.arange(length // block_len, dtype=jnp.int32) * block_len

        def one_block(entry):
            q_rows, first_row = entry
            raw_scores = jnp.dot(q_rows, k_head.T, preferred_element_type=jnp.float32) * score_scale
            q_pos = first_row + jnp.arange(block_len, dtype=jnp.int32)
            k_pos = jnp.arange(length, dtype=jnp.int32)
            masked = jnp.where(k_pos[None, :] <= q_pos[:, None], raw_scores, -jnp.inf)
            peak = lax.optimization_barrier(jnp.max(masked, axis=1))
            exp_scores = jnp.exp(masked - peak[:, None])
            row_total = lax.optimization_barrier(jnp.sum(exp_scores, axis=1))
            weights = exp_scores.astype(jnp.bfloat16)
            summed = jnp.dot(weights, v_head, preferred_element_type=jnp.float32)
            return (summed / row_total[:, None]).astype(jnp.bfloat16)
        return lax.map(one_block, (q_blocks, firsts)).reshape(length, HD)
    heads_out = lax.map(one_head, (head_q, head_k, head_v))
    attended = heads_out.reshape(HALF_HEADS, N_SEQ, QB, QROWS, HD).transpose(0, 2, 1, 3, 4).reshape(HALF_HEADS * QB, QLEN, HD)
    return (conv_mixed, attended)
```

```python
import math

import jax
import jax.numpy as jnp
from jax import lax
from jax.experimental import pallas as pl
from jax.experimental.pallas import tpu as pltpu
from jax.sharding import PartitionSpec as P

ROWS = 256
BLOCKS = 64
HD = 128
SETS = 16
QR = 16
CH = 8
LANE = 128
F32 = jnp.float32
BF16 = jnp.bfloat16
VMEM = pl.BlockSpec(memory_space=pltpu.VMEM)


def fill_toeplitz(taps_ref, gg_ref):
    row = lax.broadcasted_iota(jnp.int32, (LANE, LANE), 0)
    lane = lax.broadcasted_iota(jnp.int32, (LANE, LANE), 1)
    mask = lane >= row

    def rotated(chunk):
        line = jnp.broadcast_to(taps_ref[pl.ds(chunk, 1), :], (LANE, LANE))
        return pltpu.roll(line, 0, 1, stride=1, stride_axis=0)

    def body(d, carry):
        before, tile_before = carry
        first = rotated(2 * d)
        tile_a = jnp.where(mask, first, before).astype(BF16)
        second = rotated(2 * d + 1)
        tile_b = jnp.where(mask, second, first).astype(BF16)
        top = pl.ds(pl.multiple_of(d * 256, 256), LANE)
        low = pl.ds(pl.multiple_of(d * 256 + LANE, LANE), LANE)
        gg_ref[top, :LANE] = tile_a
        gg_ref[top, LANE:] = tile_b
        gg_ref[low, :LANE] = tile_before
        gg_ref[low, LANE:] = tile_a
        return second, tile_b

    lax.fori_loop(
        0, BLOCKS, body, (jnp.zeros((LANE, LANE), F32), jnp.zeros((LANE, LANE), BF16))
    )


def conv_kernel(taps_ref, sg_ref, skip_ref, cm_ref, gg_ref, xf_ref, xx_ref, acc_ref):
    fill_toeplitz(taps_ref, gg_ref)
    xf_ref[:64, :] = jnp.zeros((64, ROWS), F32)
    xf_ref[64:, :] = sg_ref[:, 0].astype(F32).reshape(BLOCKS * CH, ROWS)
    for e in range(8):
        xx_ref[:, e * ROWS : (e + 1) * ROWS] = xf_ref[64 - 8 * e : 576 - 8 * e, :].astype(BF16)
    acc_ref[...] = jnp.dot(xx_ref[...], gg_ref[:2048, :], preferred_element_type=F32)
    for g in range(1, 8):
        acc_ref[64 * g :, :] += jnp.dot(
            xx_ref[: 512 - 64 * g, :],
            gg_ref[2048 * g : 2048 * (g + 1), :],
            preferred_element_type=F32,
        )
    conv = acc_ref[...].reshape(BLOCKS, CH, ROWS)
    sig = sg_ref[:, 0].astype(F32)
    gate = sg_ref[:, 1].astype(F32)
    cm_ref[...] = (gate * (conv + skip_ref[...][None] * sig)).astype(BF16)


def conv_call(taps, sg, skip):
    return pl.pallas_call(
        conv_kernel,
        out_shape=jax.ShapeDtypeStruct((BLOCKS, CH, ROWS), BF16),
        in_specs=[VMEM] * 3,
        out_specs=VMEM,
        scratch_shapes=[
            pltpu.VMEM((BLOCKS * ROWS, ROWS), BF16),
            pltpu.VMEM((576, ROWS), F32),
            pltpu.VMEM((512, 2048), BF16),
            pltpu.VMEM((512, ROWS), F32),
        ],
        compiler_params=pltpu.CompilerParams(vmem_limit_bytes=50 * 2**20),
        name="conv",
    )(taps, sg, skip)


def score_tile(q_ref, k_ref, s_ref, t, my_set):
    qt = q_ref[256 * t : 256 * (t + 1), :].astype(F32).T.astype(BF16)
    qt_hi = qt[:, LANE:]

    def keys(i):
        return k_ref[:, i].reshape(ROWS, HD)

    def fold(s):
        return jnp.max(s.reshape(ROWS // 8, 8, s.shape[1]), axis=0)

    def plain(i, m):
        s = jnp.dot(keys(i), qt, preferred_element_type=F32)
        s_ref[i] = s
        return jnp.maximum(m, fold(s))

    def masked(i, width, lane0):
        s = jnp.dot(keys(i), qt if width == 256 else qt_hi, preferred_element_type=F32)
        lanes = lax.broadcasted_iota(jnp.int32, (ROWS, width), 1) + lane0
        rows = lax.broadcasted_iota(jnp.int32, (ROWS, width), 0)
        q_pos = (16 * t + lanes // QR) * ROWS + my_set * QR + lanes % QR
        return jnp.where(rows + i * ROWS <= q_pos, s, -jnp.inf)

    def diag(i, m):
        s = masked(i, 256, 0)
        s_ref[i] = s
        return jnp.maximum(m, fold(s))

    def diag_hi(i, m):
        s = masked(i, LANE, LANE)
        s_ref[i, :, LANE:] = s
        return jnp.maximum(m, fold(s))

    m = jnp.full((8, 256), -jnp.inf, F32)
    if t > 0:
        m = lax.fori_loop(0, 16 * t, plain, m, unroll=2)
    m = lax.fori_loop(16 * t, 16 * t + 8, diag, m, unroll=2)
    m_hi = lax.fori_loop(16 * t + 8, 16 * t + 16, diag_hi, m[:, LANE:], unroll=2)
    m = jnp.concatenate([m[:, :LANE], m_hi], axis=1)
    return jnp.max(m, axis=0, keepdims=True)


def attend_kernel(q_ref, k_ref, v_ref, inv_ref, out_ref, s_ref, vt_ref):
    my_set = lax.rem(lax.axis_index("seq"), SETS)
    factor = (1.0 / math.sqrt(HD)) * math.log2(math.e)

    def scale(i, carry):
        v = v_ref[:, i].astype(F32).reshape(HD, ROWS)
        vt_ref[i] = (v * inv_ref[pl.ds(i, 1), :]).astype(BF16)
        return carry

    lax.fori_loop(0, BLOCKS, scale, 0, unroll=2)
    for t in range(4):
        peak = score_tile(q_ref, k_ref, s_ref, t, my_set)

        def weigh(i, carry, wide=True):
            acc, total = carry
            s = s_ref[i] if wide else s_ref[i, :, LANE:]
            p = jnp.exp2((s - (peak if wide else peak[:, LANE:])) * factor)
            total = total + jnp.sum(p.reshape(ROWS // 8, 8, p.shape[1]), axis=0)
            acc = acc + jnp.dot(vt_ref[i], p.astype(BF16), preferred_element_type=F32)
            return acc, total

        acc, total = lax.fori_loop(
            0,
            16 * t + 8,
            weigh,
            (jnp.zeros((HD, 256), F32), jnp.zeros((8, 256), F32)),
            unroll=2,
        )
        acc_hi, total_hi = lax.fori_loop(
            16 * t + 8,
            16 * t + 16,
            lambda i, c: weigh(i, c, False),
            (acc[:, LANE:], total[:, LANE:]),
            unroll=2,
        )
        acc = jnp.concatenate([acc[:, :LANE], acc_hi], axis=1)
        total = jnp.concatenate([total[:, :LANE], total_hi], axis=1)
        total = jnp.sum(total, axis=0, keepdims=True)
        out_ref[256 * t : 256 * (t + 1), :] = (acc / total).T.astype(BF16)


def attend_call(q, k, v, inv):
    return pl.pallas_call(
        attend_kernel,
        out_shape=jax.ShapeDtypeStruct((BLOCKS * QR, HD), BF16),
        in_specs=[VMEM] * 4,
        out_specs=VMEM,
        scratch_shapes=[
            pltpu.VMEM((BLOCKS, ROWS, 256), F32),
            pltpu.VMEM((BLOCKS, HD, ROWS), BF16),
        ],
        compiler_params=pltpu.CompilerParams(vmem_limit_bytes=50 * 2**20),
        name="attend",
    )(q, k, v, inv)


def shards(signal, gate_rows, skip_gain, filter_taps, queries, key_rows):
    me = lax.axis_index("seq")
    head = me // SETS
    heads_loc = filter_taps.shape[1]
    groups = [[h * SETS + b for b in range(SETS)] for h in range(heads_loc)]

    def split_rows(x):
        return (
            x.reshape(SETS, QR, heads_loc, HD).transpose(2, 0, 1, 3).reshape(BLOCKS, 1, QR, HD)
        )

    def split_channels(x):
        return x.T.reshape(BLOCKS, 1, CH, ROWS)

    sg = jnp.concatenate([split_channels(signal), split_channels(gate_rows)], axis=1)
    qk = jnp.concatenate([split_rows(queries), split_rows(key_rows)], axis=1)
    sg = lax.all_to_all(sg, "seq", split_axis=0, concat_axis=0, tiled=True)
    qk = lax.all_to_all(qk, "seq", split_axis=0, concat_axis=0, tiled=True)
    k_all = lax.all_gather(qk[:, 1], "seq", axis=0, tiled=False, axis_index_groups=groups)
    taps = lax.dynamic_slice_in_dim(filter_taps.T, head, 1, 0).reshape(LANE, LANE).astype(F32)
    skip = jnp.broadcast_to(lax.dynamic_slice_in_dim(skip_gain, me * CH, CH)[:, None], (CH, ROWS))
    cm = conv_call(taps, sg, skip)
    cm_all = lax.all_gather(cm, "seq", axis=0, tiled=False, axis_index_groups=groups)
    home = lax.all_to_all(cm, "seq", split_axis=0, concat_axis=0, tiled=True)
    home = home.reshape(BLOCKS * CH, ROWS)
    squares = jnp.sum(jnp.square(home.astype(F32)), axis=0)
    whole = lax.psum(squares, "chan")
    inv = lax.rsqrt(whole / (heads_loc * HD * lax.axis_size("chan")) + 1e-06)
    inv_all = lax.all_gather(inv, "seq", axis=0, tiled=False)
    attended = attend_call(qk[:, 0].reshape(BLOCKS * QR, HD), k_all, cm_all, inv_all)
    return home.T, attended[None]


def solution(mesh):
    in_specs = (
        P("seq", "chan"),
        P("seq", "chan"),
        P("chan"),
        P(None, "chan"),
        P("seq", "chan"),
        P("seq", "chan"),
    )
    out_specs = (P("seq", "chan"), P(("chan", "seq"), None, None))
    return jax.shard_map(shards, mesh=mesh, in_specs=in_specs, out_specs=out_specs, check_vma=False)
```

```python
import math

import jax
import jax.numpy as jnp
from jax import lax
from jax.experimental import pallas as pl
from jax.experimental.pallas import tpu as pltpu
from jax.sharding import PartitionSpec as P

ROWS = 256
BLOCKS = 64
HD = 128
SETS = 16
QR = 16
CH = 8
LANE = 128
F32 = jnp.float32
BF16 = jnp.bfloat16
MESH = pl.DeviceIdType.MESH
VMEM = pl.BlockSpec(memory_space=pltpu.VMEM)


def fill_toeplitz(taps_ref, gg_ref):
    row = lax.broadcasted_iota(jnp.int32, (LANE, LANE), 0)
    lane = lax.broadcasted_iota(jnp.int32, (LANE, LANE), 1)
    mask = lane >= row

    def rotated(chunk):
        line = jnp.broadcast_to(taps_ref[pl.ds(chunk, 1), :], (LANE, LANE))
        return pltpu.roll(line, 0, 1, stride=1, stride_axis=0)

    def body(d, carry):
        before, tile_before = carry
        first = rotated(2 * d)
        tile_a = jnp.where(mask, first, before).astype(BF16)
        second = rotated(2 * d + 1)
        tile_b = jnp.where(mask, second, first).astype(BF16)
        top = pl.ds(pl.multiple_of(d * 256, 256), LANE)
        low = pl.ds(pl.multiple_of(d * 256 + LANE, LANE), LANE)
        gg_ref[top, :LANE] = tile_a
        gg_ref[top, LANE:] = tile_b
        gg_ref[low, :LANE] = tile_before
        gg_ref[low, LANE:] = tile_a
        return second, tile_b

    lax.fori_loop(
        0, BLOCKS, body, (jnp.zeros((LANE, LANE), F32), jnp.zeros((LANE, LANE), BF16))
    )


def landed(ref, sem):
    pltpu.make_async_copy(ref, ref, sem).wait()


def fold_rows(x, op):
    return op(x.reshape(x.shape[0] // 8, 8, x.shape[1]), axis=0)


def tile_base(slot, t):
    return slot * 80 + 4 * t * (t + 1)


def mega_kernel(
    sig_ref, gate_ref, taps_ref, skip_ref, q_ref, k_ref,
    mixed_ref, out_ref,
    st_s, st_g, rs, rg, qb, kb, cmh, hb, vb, sq_out, sq_in, inv_out, inv_in,
    gg, xf, xx, acc_ref, s_ref, p_ref, vt_ref, stat, ob_out, ob_in, os_out, os_in,
    a_send, a_recv, k_send, k_recv, v_send, v_recv, o_send, o_recv,
):
    seq_count = lax.axis_size("seq")
    chan_count = lax.axis_size("chan")
    me = lax.axis_index("seq")
    my_chan = lax.axis_index("chan")
    core = me % 2
    y = (me // 2) % 4
    row0 = (me // 8) * 8
    zr = (me // 8) % 2
    my_set = me % SETS
    my_slot = me % 8
    other_core = me + 1 - 2 * core
    across = me + 8 - 16 * zr
    row1 = row0 + 8 - 16 * zr
    factor = (1.0 / math.sqrt(HD)) * math.log2(math.e)

    def send(src, dst, s_sem, r_sem, where):
        pltpu.make_async_remote_copy(
            src_ref=src, dst_ref=dst, send_sem=s_sem, recv_sem=r_sem,
            device_id=where, device_id_type=MESH,
        ).start()

    def others(body):
        def step(n, carry):
            body((me + n) % seq_count)
            return carry

        lax.fori_loop(1, seq_count, step, 0)

    def piece(ref, d):
        rows = pl.ds(pl.multiple_of((d % SETS) * QR, QR), QR)
        return ref.at[rows, pl.ds(pl.multiple_of((d // SETS) * HD, HD), HD)]

    def flip(d):
        return d + 8 - 16 * ((d // 8) % 2)

    st_s[...] = sig_ref[...].astype(F32).T.reshape(BLOCKS, CH, ROWS).astype(BF16)
    st_g[...] = gate_ref[...].astype(F32).T.reshape(BLOCKS, CH, ROWS).astype(BF16)

    barrier = pltpu.get_barrier_semaphore()
    others(
        lambda d: pl.semaphore_signal(
            barrier, inc=1, device_id={"seq": d}, device_id_type=MESH
        )
    )
    for n in range(1, chan_count):
        pl.semaphore_signal(
            barrier, inc=1, device_id={"chan": (my_chan + n) % chan_count}, device_id_type=MESH
        )
    pl.semaphore_wait(barrier, seq_count + chan_count - 2)

    others(lambda d: send(st_s.at[d], rs.at[me], a_send.at[0], a_recv.at[0], {"seq": d}))
    others(
        lambda d: send(
            piece(k_ref, d), kb.at[d % 8, me], a_send.at[1], a_recv.at[1], {"seq": d}
        )
    )
    others(lambda d: send(st_g.at[d], rg.at[me], a_send.at[2], a_recv.at[2], {"seq": d}))

    def send_queries(d):
        send(piece(q_ref, flip(d)), qb.at[1, me], a_send.at[3], a_recv.at[3], {"seq": d})
        send(piece(q_ref, d), qb.at[0, me], a_send.at[4], a_recv.at[4], {"seq": d})

    others(send_queries)
    rs[me] = st_s[me]
    rg[me] = st_g[me]
    kb[my_slot, me] = piece(k_ref, me)[...]
    qb[0, me] = piece(q_ref, me)[...]
    qb[1, me] = piece(q_ref, across)[...]

    fill_toeplitz(taps_ref, gg)
    xf[:64, :] = jnp.zeros((64, ROWS), F32)
    landed(rs.at[pl.ds(0, 63)], a_recv.at[0])
    xf[64:, :] = rs[...].astype(F32).reshape(BLOCKS * CH, ROWS)
    for e in range(8):
        xx[:, e * ROWS : (e + 1) * ROWS] = xf[64 - 8 * e : 576 - 8 * e, :].astype(BF16)
    acc_ref[...] = jnp.dot(xx[...], gg[:2048, :], preferred_element_type=F32)
    for g in range(1, 8):
        acc_ref[64 * g :, :] += jnp.dot(
            xx[: 512 - 64 * g, :],
            gg[2048 * g : 2048 * (g + 1), :],
            preferred_element_type=F32,
        )

    landed(kb.at[0, pl.ds(0, 63)], a_recv.at[1])
    row_mates = [row0 + ((y + n) % 4) * 2 + core for n in range(4)]
    far_mates = [row1 + ((y + n) % 4) * 2 + core for n in range(4)]
    for n in (1, 3, 2):
        send(
            kb.at[my_slot], kb.at[my_slot], k_send.at[n], k_recv.at[my_slot],
            {"seq": row_mates[n]},
        )
    send(kb.at[my_slot], kb.at[my_slot], k_send.at[0], k_recv.at[my_slot], {"seq": other_core})

    landed(rg.at[pl.ds(0, 63)], a_recv.at[2])
    conv = acc_ref[...].reshape(BLOCKS, CH, ROWS)
    mixed = rg[...].astype(F32) * (conv + skip_ref[...][None] * rs[...].astype(F32))
    mixed = mixed.astype(BF16)
    cmh[0] = mixed[:, :, :LANE]
    cmh[1] = mixed[:, :, LANE:]
    others(lambda d: send(cmh.at[:, d], hb.at[me], a_send.at[5], a_recv.at[5], {"seq": d}))
    hb[me] = cmh[:, me]
    vb[my_set] = cmh[zr]
    for n in range(4):
        where = other_core if n == 0 else row_mates[n]
        send(cmh.at[zr], vb.at[my_set], v_send.at[n], v_recv.at[my_set], {"seq": where})
    for n in range(4):
        send(
            cmh.at[1 - zr], vb.at[my_set], v_send.at[4 + n], v_recv.at[my_set],
            {"seq": far_mates[n]},
        )

    landed(hb.at[pl.ds(0, 63)], a_recv.at[5])
    for half in range(2):
        lanes = slice(half * LANE, (half + 1) * LANE)
        wide = hb[:, half].astype(F32).reshape(BLOCKS * CH, LANE)
        sq_out[:, lanes] = jnp.sum(fold_rows(wide * wide, jnp.sum), axis=0, keepdims=True)
    sq_in[my_chan] = sq_out[...]
    for n in range(1, chan_count):
        send(
            sq_out, sq_in.at[my_chan], o_send.at[8 + n], a_recv.at[6],
            {"chan": (my_chan + n) % chan_count},
        )
    for half in range(2):
        wide = hb[:, half].astype(F32).reshape(BLOCKS * CH, LANE)
        mixed_ref[half * LANE : (half + 1) * LANE, :] = wide.T.astype(BF16)
    if chan_count > 1:
        landed(sq_in.at[pl.ds(0, chan_count - 1)], a_recv.at[6])
    whole = sq_in[0]
    for n in range(1, chan_count):
        whole = whole + sq_in[n]
    inv_out[...] = lax.rsqrt(whole / (BLOCKS * CH * chan_count) + 1e-06)
    others(lambda d: send(inv_out, inv_in.at[me], a_send.at[6], a_recv.at[7], {"seq": d}))
    inv_in[me] = inv_out[...]

    for n in (1, 3, 2):
        slot = row_mates[n] % 8
        landed(kb.at[slot], k_recv.at[slot])
        send(kb.at[slot], kb.at[slot], k_send.at[3 + n], k_recv.at[slot], {"seq": other_core})
    for n in range(4):
        slot = row_mates[n] % 8 + 1 - 2 * core
        landed(kb.at[slot], k_recv.at[slot])

    def scores(slot):
        bq = (my_set + 8 * slot) % SETS

        def tile(t, carry):
            base = tile_base(slot, t)
            q = qb[slot, pl.ds(t * SETS, SETS)].reshape(256, HD)
            qt = q.astype(F32).T.astype(BF16)
            qt_hi = qt[:, LANE:]

            def keys(p):
                return jnp.concatenate(
                    [kb[:, 2 * p].reshape(LANE, HD), kb[:, 2 * p + 1].reshape(LANE, HD)], axis=0
                )

            def plain(u, m):
                for p in (2 * u, 2 * u + 1):
                    s = jnp.dot(keys(p), qt, preferred_element_type=F32)
                    s_ref[p] = s
                    m = jnp.maximum(m, fold_rows(s, jnp.max))
                return m

            def masked(p, width, lane0):
                s = jnp.dot(
                    keys(p), qt if width == 256 else qt_hi, preferred_element_type=F32
                )
                lanes = lax.broadcasted_iota(jnp.int32, (256, width), 1) + lane0
                rows = lax.broadcasted_iota(jnp.int32, (256, width), 0)
                q_pos = (lanes // QR) * ROWS + lanes % QR
                k_pos = (rows // LANE) * ROWS + rows % LANE
                shift = 16 * t * ROWS + bq * QR - 2 * p * ROWS - zr * LANE
                return jnp.where(k_pos - q_pos <= shift, s, -1e30)

            def diag(u, m):
                p = 8 * t + u
                s = masked(p, 256, 0)
                s_ref[p] = s
                return jnp.maximum(m, fold_rows(s, jnp.max))

            def diag_hi(u, m):
                p = 8 * t + 4 + u
                s = masked(p, LANE, LANE)
                s_ref[p, :, LANE:] = s
                return jnp.maximum(m, fold_rows(s, jnp.max))

            m = jnp.full((8, 256), -1e30, F32)
            m = lax.fori_loop(0, 4 * t, plain, m)
            m = lax.fori_loop(0, 4, diag, m, unroll=2)
            m_hi = lax.fori_loop(0, 4, diag_hi, m[:, LANE:], unroll=2)
            m = jnp.concatenate([m[:, :LANE], m_hi], axis=1)
            peak = jnp.max(m, axis=0, keepdims=True)

            def weigh(p, total):
                w = jnp.exp2((s_ref[p] - peak) * factor)
                p_ref[base + p] = w.astype(BF16)
                return total + fold_rows(w, jnp.sum)

            def weigh_two(u, total):
                return weigh(2 * u + 1, weigh(2 * u, total))

            def weigh_hi(u, total):
                p = 8 * t + 4 + u
                w = jnp.exp2((s_ref[p, :, LANE:] - peak[:, LANE:]) * factor)
                p_ref[base + p, :, LANE:] = w.astype(BF16)
                return total + fold_rows(w, jnp.sum)

            total = lax.fori_loop(0, 4 * t + 2, weigh_two, jnp.zeros((8, 256), F32))
            total_hi = lax.fori_loop(0, 4, weigh_hi, total[:, LANE:], unroll=2)
            total = jnp.concatenate([total[:, :LANE], total_hi], axis=1)
            stat[slot, t, :8] = jnp.broadcast_to(peak, (8, 256))
            stat[slot, t, 8:] = jnp.broadcast_to(
                jnp.sum(total, axis=0, keepdims=True), (8, 256)
            )
            return carry

        lax.fori_loop(0, 4, tile, 0)

    def weighted(slot, t):
        base = tile_base(slot, t)

        def both(u, acc):
            for p in (2 * u, 2 * u + 1):
                acc = acc + jnp.dot(vt_ref[p], p_ref[base + p], preferred_element_type=F32)
            return acc

        def high(u, acc):
            p = 8 * t + 4 + u
            return acc + jnp.dot(
                vt_ref[p], p_ref[base + p, :, LANE:], preferred_element_type=F32
            )

        acc = lax.fori_loop(0, 4 * t + 2, both, jnp.zeros((HD, 256), F32))
        acc_hi = lax.fori_loop(0, 4, high, acc[:, LANE:], unroll=2)
        return jnp.concatenate([acc[:, :LANE], acc_hi], axis=1)

    landed(qb.at[1, pl.ds(0, 63)], a_recv.at[3])
    scores(1)
    for n in (4, 1, 3, 5, 7, 2, 6):
        slot = (row_mates[n] if n < 4 else far_mates[n - 4]) % SETS
        landed(vb.at[slot], v_recv.at[slot])
        send(vb.at[slot], vb.at[slot], v_send.at[7 + n], v_recv.at[slot], {"seq": other_core})
    landed(qb.at[0, pl.ds(0, 63)], a_recv.at[4])
    scores(0)

    for n in range(8):
        slot = (row_mates[n] if n < 4 else far_mates[n - 4]) % SETS + 1 - 2 * core
        landed(vb.at[slot], v_recv.at[slot])
    landed(inv_in.at[pl.ds(0, 63)], a_recv.at[7])

    def scale(p, carry):
        for u in range(2):
            v = vb[:, 2 * p + u].astype(F32).reshape(HD, LANE)
            inv = inv_in[2 * p + u, :, pl.ds(pl.multiple_of(zr * LANE, LANE), LANE)]
            vt_ref[p, :, u * LANE : (u + 1) * LANE] = (v * inv).astype(BF16)
        return carry

    lax.fori_loop(0, BLOCKS // 2, scale, 0)

    def help_tile(u, carry):
        t = 3 - u
        acc = weighted(1, t)
        ob_out[t] = (acc / stat[1, t, 8:9]).astype(BF16)
        send(ob_out.at[t], ob_in.at[t], o_send.at[t], o_recv.at[t], {"seq": across})
        send(stat.at[1, t], os_in.at[t], o_send.at[4 + t], o_recv.at[4 + t], {"seq": across})
        return carry

    lax.fori_loop(0, 4, help_tile, 0)

    def own_tile(u, carry):
        t = 3 - u
        acc = weighted(0, t)
        landed(ob_in.at[t], o_recv.at[t])
        landed(os_in.at[t], o_recv.at[4 + t])
        m0, m1 = stat[0, t, 0:1], os_in[t, 0:1]
        top = jnp.maximum(m0, m1)
        w0 = jnp.exp2((m0 - top) * factor)
        w1 = os_in[t, 8:9] * jnp.exp2((m1 - top) * factor)
        total = stat[0, t, 8:9] * w0 + w1
        merged = (acc * w0 + ob_in[t].astype(F32) * w1) / total
        out_ref[pl.ds(pl.multiple_of(t * 256, 256), 256), :] = merged.T.astype(BF16)
        return carry

    lax.fori_loop(0, 4, own_tile, 0)

    landed(rs.at[pl.ds(0, 63)], a_send.at[0])
    landed(kb.at[0, pl.ds(0, 63)], a_send.at[1])
    landed(rg.at[pl.ds(0, 63)], a_send.at[2])
    landed(qb.at[1, pl.ds(0, 63)], a_send.at[3])
    landed(qb.at[0, pl.ds(0, 63)], a_send.at[4])
    landed(hb.at[pl.ds(0, 63)], a_send.at[5])
    landed(inv_in.at[pl.ds(0, 63)], a_send.at[6])
    for n in range(7):
        landed(kb.at[0], k_send.at[n])
    for n in range(15):
        landed(vb.at[0], v_send.at[n])
    for t in range(4):
        landed(ob_in.at[t], o_send.at[t])
        landed(os_in.at[t], o_send.at[4 + t])
    for n in range(1, chan_count):
        landed(sq_in.at[0], o_send.at[8 + n])


def mega_call(sig, gate, taps, skip, q, k):
    return pl.pallas_call(
        mega_kernel,
        out_shape=(
            jax.ShapeDtypeStruct((ROWS, BLOCKS * CH), BF16),
            jax.ShapeDtypeStruct((BLOCKS * QR, HD), BF16),
        ),
        in_specs=[VMEM] * 6,
        out_specs=(VMEM, VMEM),
        scratch_shapes=[
            pltpu.VMEM((BLOCKS, CH, ROWS), BF16),
            pltpu.VMEM((BLOCKS, CH, ROWS), BF16),
            pltpu.VMEM((BLOCKS, CH, ROWS), BF16),
            pltpu.VMEM((BLOCKS, CH, ROWS), BF16),
            pltpu.VMEM((2, BLOCKS, QR, HD), BF16),
            pltpu.VMEM((8, BLOCKS, QR, HD), BF16),
            pltpu.VMEM((2, BLOCKS, CH, LANE), BF16),
            pltpu.VMEM((BLOCKS, 2, CH, LANE), BF16),
            pltpu.VMEM((SETS, BLOCKS, CH, LANE), BF16),
            pltpu.VMEM((1, ROWS), F32),
            pltpu.VMEM((4, 1, ROWS), F32),
            pltpu.VMEM((1, ROWS), F32),
            pltpu.VMEM((BLOCKS, 1, ROWS), F32),
            pltpu.VMEM((BLOCKS * ROWS, ROWS), BF16),
            pltpu.VMEM((576, ROWS), F32),
            pltpu.VMEM((512, 2048), BF16),
            pltpu.VMEM((512, ROWS), F32),
            pltpu.VMEM((BLOCKS // 2, 256, 256), F32),
            pltpu.VMEM((160, 256, 256), BF16),
            pltpu.VMEM((BLOCKS // 2, HD, 256), BF16),
            pltpu.VMEM((2, 4, 16, 256), F32),
            pltpu.VMEM((4, HD, 256), BF16),
            pltpu.VMEM((4, HD, 256), BF16),
            pltpu.VMEM((4, 16, 256), F32),
            pltpu.VMEM((4, 16, 256), F32),
            pltpu.SemaphoreType.DMA((7,)),
            pltpu.SemaphoreType.DMA((8,)),
            pltpu.SemaphoreType.DMA((7,)),
            pltpu.SemaphoreType.DMA((8,)),
            pltpu.SemaphoreType.DMA((15,)),
            pltpu.SemaphoreType.DMA((16,)),
            pltpu.SemaphoreType.DMA((12,)),
            pltpu.SemaphoreType.DMA((8,)),
        ],
        compiler_params=pltpu.CompilerParams(
            vmem_limit_bytes=62 * 2**20, collective_id=0, has_side_effects=True
        ),
        name="mega",
    )(sig, gate, taps, skip, q, k)


def shards(signal, gate_rows, skip_gain, filter_taps, queries, key_rows):
    me = lax.axis_index("seq")
    taps = lax.dynamic_slice_in_dim(filter_taps.T, me // SETS, 1, 0)
    taps = taps.reshape(LANE, LANE).astype(F32)
    skip = jnp.broadcast_to(lax.dynamic_slice_in_dim(skip_gain, me * CH, CH)[:, None], (CH, ROWS))
    mixed, attended = mega_call(signal, gate_rows, taps, skip, queries, key_rows)
    return mixed, attended[None]


def solution(mesh):
    in_specs = (
        P("seq", "chan"),
        P("seq", "chan"),
        P("chan"),
        P(None, "chan"),
        P("seq", "chan"),
        P("seq", "chan"),
    )
    out_specs = (P("seq", "chan"), P(("chan", "seq"), None, None))
    return jax.shard_map(shards, mesh=mesh, in_specs=in_specs, out_specs=out_specs, check_vma=False)
```

```python
import math

import jax
import jax.numpy as jnp
from jax import lax
from jax.experimental import pallas as pl
from jax.experimental.pallas import tpu as pltpu
from jax.sharding import PartitionSpec as P

ROWS = 256
BLOCKS = 64
HD = 128
SETS = 16
QR = 16
CH = 8
LANE = 128
F32 = jnp.float32
BF16 = jnp.bfloat16
MESH = pl.DeviceIdType.MESH
VMEM = pl.BlockSpec(memory_space=pltpu.VMEM)


def fill_toeplitz(taps_ref, gg_ref):
    row = lax.broadcasted_iota(jnp.int32, (LANE, LANE), 0)
    lane = lax.broadcasted_iota(jnp.int32, (LANE, LANE), 1)
    mask = lane >= row

    def rotated(chunk):
        line = jnp.broadcast_to(taps_ref[pl.ds(chunk, 1), :], (LANE, LANE))
        return pltpu.roll(line, 0, 1, stride=1, stride_axis=0)

    def body(d, carry):
        before, tile_before = carry
        first = rotated(2 * d)
        tile_a = jnp.where(mask, first, before).astype(BF16)
        second = rotated(2 * d + 1)
        tile_b = jnp.where(mask, second, first).astype(BF16)
        top = pl.ds(pl.multiple_of(d * 256, 256), LANE)
        low = pl.ds(pl.multiple_of(d * 256 + LANE, LANE), LANE)
        gg_ref[top, :LANE] = tile_a
        gg_ref[top, LANE:] = tile_b
        gg_ref[low, :LANE] = tile_before
        gg_ref[low, LANE:] = tile_a
        return second, tile_b

    lax.fori_loop(
        0, BLOCKS, body, (jnp.zeros((LANE, LANE), F32), jnp.zeros((LANE, LANE), BF16))
    )


def landed(ref, sem):
    pltpu.make_async_copy(ref, ref, sem).wait()


def fold_rows(x, op):
    return op(x.reshape(x.shape[0] // 8, 8, x.shape[1]), axis=0)


def tile_base(slot, t):
    return slot * 80 + 4 * t * (t + 1)


def mega_kernel(
    sig_ref, gate_ref, taps_ref, skip_ref, q_ref, k_ref,
    mixed_ref, out_ref,
    st_s, st_g, rs, rg, qb, kb, cmh, hb, vb, sq_out, sq_in, inv_out, inv_in,
    gg, xf, xx, acc_ref, s_ref, p_ref, vt_ref, stat, ob_out, ob_in, os_out, os_in,
    a_send, a_recv, k_send, k_recv, v_send, v_recv, o_send, o_recv,
):
    seq_count = lax.axis_size("seq")
    chan_count = lax.axis_size("chan")
    me = lax.axis_index("seq")
    my_chan = lax.axis_index("chan")
    core = me % 2
    y = (me // 2) % 4
    row0 = (me // 8) * 8
    zr = (me // 8) % 2
    my_set = me % SETS
    my_slot = me % 8
    other_core = me + 1 - 2 * core
    across = me + 8 - 16 * zr
    row1 = row0 + 8 - 16 * zr
    factor = (1.0 / math.sqrt(HD)) * math.log2(math.e)

    def send(src, dst, s_sem, r_sem, where):
        pltpu.make_async_remote_copy(
            src_ref=src, dst_ref=dst, send_sem=s_sem, recv_sem=r_sem,
            device_id=where, device_id_type=MESH,
        ).start()

    def others(body):
        def step(n, carry):
            body((me + n) % seq_count)
            return carry

        lax.fori_loop(1, seq_count, step, 0)

    def piece(ref, d):
        rows = pl.ds(pl.multiple_of((d % SETS) * QR, QR), QR)
        return ref.at[rows, pl.ds(pl.multiple_of((d // SETS) * HD, HD), HD)]

    st_s[...] = sig_ref[...].astype(F32).T.reshape(BLOCKS, CH, ROWS).astype(BF16)
    st_g[...] = gate_ref[...].astype(F32).T.reshape(BLOCKS, CH, ROWS).astype(BF16)

    barrier = pltpu.get_barrier_semaphore()
    others(
        lambda d: pl.semaphore_signal(
            barrier, inc=1, device_id={"seq": d}, device_id_type=MESH
        )
    )
    for n in range(1, chan_count):
        pl.semaphore_signal(
            barrier, inc=1, device_id={"chan": (my_chan + n) % chan_count}, device_id_type=MESH
        )
    pl.semaphore_wait(barrier, seq_count + chan_count - 2)

    others(lambda d: send(st_s.at[d], rs.at[me], a_send.at[0], a_recv.at[0], {"seq": d}))
    others(
        lambda d: send(
            piece(k_ref, d), kb.at[d % 8, me], a_send.at[1], a_recv.at[1], {"seq": d}
        )
    )
    others(lambda d: send(st_g.at[d], rg.at[me], a_send.at[2], a_recv.at[2], {"seq": d}))

    others(
        lambda d: send(
            piece(q_ref, d), qb.at[0, me], a_send.at[4], a_recv.at[4], {"seq": d}
        )
    )
    rs[me] = st_s[me]
    rg[me] = st_g[me]
    kb[my_slot, me] = piece(k_ref, me)[...]
    qb[0, me] = piece(q_ref, me)[...]

    fill_toeplitz(taps_ref, gg)
    xf[:64, :] = jnp.zeros((64, ROWS), F32)
    landed(rs.at[pl.ds(0, 63)], a_recv.at[0])
    xf[64:, :] = rs[...].astype(F32).reshape(BLOCKS * CH, ROWS)
    for e in range(8):
        xx[:, e * ROWS : (e + 1) * ROWS] = xf[64 - 8 * e : 576 - 8 * e, :].astype(BF16)
    acc_ref[...] = jnp.dot(xx[...], gg[:2048, :], preferred_element_type=F32)
    for g in range(1, 8):
        acc_ref[64 * g :, :] += jnp.dot(
            xx[: 512 - 64 * g, :],
            gg[2048 * g : 2048 * (g + 1), :],
            preferred_element_type=F32,
        )

    landed(kb.at[0, pl.ds(0, 63)], a_recv.at[1])
    row_mates = [row0 + ((y + n) % 4) * 2 + core for n in range(4)]
    far_mates = [row1 + ((y + n) % 4) * 2 + core for n in range(4)]
    for n in (1, 3, 2):
        send(
            kb.at[my_slot], kb.at[my_slot], k_send.at[n], k_recv.at[my_slot],
            {"seq": row_mates[n]},
        )
    send(kb.at[my_slot], kb.at[my_slot], k_send.at[0], k_recv.at[my_slot], {"seq": other_core})

    landed(rg.at[pl.ds(0, 63)], a_recv.at[2])
    conv = acc_ref[...].reshape(BLOCKS, CH, ROWS)
    mixed = rg[...].astype(F32) * (conv + skip_ref[...][None] * rs[...].astype(F32))
    mixed = mixed.astype(BF16)
    cmh[0] = mixed[:, :, :LANE]
    cmh[1] = mixed[:, :, LANE:]
    others(lambda d: send(cmh.at[:, d], hb.at[me], a_send.at[5], a_recv.at[5], {"seq": d}))
    hb[me] = cmh[:, me]
    send(cmh.at[1 - zr], vb.at[my_set], v_send.at[4], v_recv.at[my_set], {"seq": across})
    vb[my_set] = cmh[zr]
    for n in range(4):
        where = other_core if n == 0 else row_mates[n]
        send(cmh.at[zr], vb.at[my_set], v_send.at[n], v_recv.at[my_set], {"seq": where})

    for n in (1, 3, 2):
        slot = row_mates[n] % 8
        landed(kb.at[slot], k_recv.at[slot])
        send(kb.at[slot], kb.at[slot], k_send.at[3 + n], k_recv.at[slot], {"seq": other_core})
    for n in range(4):
        slot = row_mates[n] % 8 + 1 - 2 * core
        landed(kb.at[slot], k_recv.at[slot])

    def scores(slot, first, last):
        bq = (my_set + 8 * slot) % SETS

        def tile(t, carry):
            base = tile_base(slot, t)
            q = qb[slot, pl.ds(t * SETS, SETS)].reshape(256, HD)
            qt = q.astype(F32).T.astype(BF16)
            qt_hi = qt[:, LANE:]

            def keys(p):
                return jnp.concatenate(
                    [kb[:, 2 * p].reshape(LANE, HD), kb[:, 2 * p + 1].reshape(LANE, HD)], axis=0
                )

            def plain(u, m):
                for p in (2 * u, 2 * u + 1):
                    s = jnp.dot(keys(p), qt, preferred_element_type=F32)
                    s_ref[p] = s
                    m = jnp.maximum(m, fold_rows(s, jnp.max))
                return m

            def masked(p, width, lane0):
                s = jnp.dot(
                    keys(p), qt if width == 256 else qt_hi, preferred_element_type=F32
                )
                lanes = lax.broadcasted_iota(jnp.int32, (256, width), 1) + lane0
                rows = lax.broadcasted_iota(jnp.int32, (256, width), 0)
                q_pos = (lanes // QR) * ROWS + lanes % QR
                k_pos = (rows // LANE) * ROWS + rows % LANE
                shift = 16 * t * ROWS + bq * QR - 2 * p * ROWS - zr * LANE
                return jnp.where(k_pos - q_pos <= shift, s, -1e30)

            def diag(u, m):
                p = 8 * t + u
                s = masked(p, 256, 0)
                s_ref[p] = s
                return jnp.maximum(m, fold_rows(s, jnp.max))

            def diag_hi(u, m):
                p = 8 * t + 4 + u
                s = masked(p, LANE, LANE)
                s_ref[p, :, LANE:] = s
                return jnp.maximum(m, fold_rows(s, jnp.max))

            m = jnp.full((8, 256), -1e30, F32)
            m = lax.fori_loop(0, 4 * t, plain, m)
            m = lax.fori_loop(0, 4, diag, m, unroll=2)
            m_hi = lax.fori_loop(0, 4, diag_hi, m[:, LANE:], unroll=2)
            m = jnp.concatenate([m[:, :LANE], m_hi], axis=1)
            peak = jnp.max(m, axis=0, keepdims=True)

            def weigh(p, total):
                w = jnp.exp2((s_ref[p] - peak) * factor)
                p_ref[base + p] = w.astype(BF16)
                return total + fold_rows(w, jnp.sum)

            def weigh_two(u, total):
                return weigh(2 * u + 1, weigh(2 * u, total))

            def weigh_hi(u, total):
                p = 8 * t + 4 + u
                w = jnp.exp2((s_ref[p, :, LANE:] - peak[:, LANE:]) * factor)
                p_ref[base + p, :, LANE:] = w.astype(BF16)
                return total + fold_rows(w, jnp.sum)

            total = lax.fori_loop(0, 4 * t + 2, weigh_two, jnp.zeros((8, 256), F32))
            total_hi = lax.fori_loop(0, 4, weigh_hi, total[:, LANE:], unroll=2)
            total = jnp.concatenate([total[:, :LANE], total_hi], axis=1)
            stat[slot, t, :8] = jnp.broadcast_to(peak, (8, 256))
            stat[slot, t, 8:] = jnp.broadcast_to(
                jnp.sum(total, axis=0, keepdims=True), (8, 256)
            )
            return carry

        lax.fori_loop(first, last, tile, 0)

    def weighted(slot, t):
        base = tile_base(slot, t)

        def both(u, acc):
            for p in (2 * u, 2 * u + 1):
                acc = acc + jnp.dot(vt_ref[p], p_ref[base + p], preferred_element_type=F32)
            return acc

        def high(u, acc):
            p = 8 * t + 4 + u
            return acc + jnp.dot(
                vt_ref[p], p_ref[base + p, :, LANE:], preferred_element_type=F32
            )

        acc = lax.fori_loop(0, 4 * t + 2, both, jnp.zeros((HD, 256), F32))
        acc_hi = lax.fori_loop(0, 4, high, acc[:, LANE:], unroll=2)
        return jnp.concatenate([acc[:, :LANE], acc_hi], axis=1)

    def pass_values(n):
        slot = (row_mates[n] if n < 4 else far_mates[n - 4]) % SETS
        landed(vb.at[slot], v_recv.at[slot])
        send(vb.at[slot], vb.at[slot], v_send.at[8 + n - n // 4], v_recv.at[slot], {"seq": other_core})

    landed(qb.at[0, pl.ds(0, 63)], a_recv.at[4])
    send(qb.at[0], qb.at[1], a_send.at[3], a_recv.at[3], {"seq": across})
    scores(0, 0, 3)

    landed(hb.at[pl.ds(0, 63)], a_recv.at[5])
    for half in range(2):
        lanes = slice(half * LANE, (half + 1) * LANE)
        wide = hb[:, half].astype(F32).reshape(BLOCKS * CH, LANE)
        sq_out[:, lanes] = jnp.sum(fold_rows(wide * wide, jnp.sum), axis=0, keepdims=True)
    sq_in[my_chan] = sq_out[...]
    for n in range(1, chan_count):
        send(
            sq_out, sq_in.at[my_chan], o_send.at[8 + n], a_recv.at[6],
            {"chan": (my_chan + n) % chan_count},
        )
    for half in range(2):
        wide = hb[:, half].astype(F32).reshape(BLOCKS * CH, LANE)
        mixed_ref[half * LANE : (half + 1) * LANE, :] = wide.T.astype(BF16)

    far = across % SETS
    landed(vb.at[far], v_recv.at[far])
    for n in (1, 3, 2):
        send(vb.at[far], vb.at[far], v_send.at[4 + n], v_recv.at[far], {"seq": row_mates[n]})
    send(vb.at[far], vb.at[far], v_send.at[8], v_recv.at[far], {"seq": other_core})
    scores(0, 3, 4)

    if chan_count > 1:
        landed(sq_in.at[pl.ds(0, chan_count - 1)], a_recv.at[6])
    whole = sq_in[0]
    for n in range(1, chan_count):
        whole = whole + sq_in[n]
    inv_out[...] = lax.rsqrt(whole / (BLOCKS * CH * chan_count) + 1e-06)
    others(lambda d: send(inv_out, inv_in.at[me], a_send.at[6], a_recv.at[7], {"seq": d}))
    inv_in[me] = inv_out[...]

    for n in (1, 3, 2):
        pass_values(n)
    landed(qb.at[1], a_recv.at[3])
    scores(1, 0, 3)
    for n in (5, 7, 6):
        pass_values(n)
    scores(1, 3, 4)

    for n in range(8):
        slot = (row_mates[n] if n < 4 else far_mates[n - 4]) % SETS + 1 - 2 * core
        landed(vb.at[slot], v_recv.at[slot])
    landed(inv_in.at[pl.ds(0, 63)], a_recv.at[7])

    def scale(p, carry):
        for u in range(2):
            v = vb[:, 2 * p + u].astype(F32).reshape(HD, LANE)
            inv = inv_in[2 * p + u, :, pl.ds(pl.multiple_of(zr * LANE, LANE), LANE)]
            vt_ref[p, :, u * LANE : (u + 1) * LANE] = (v * inv).astype(BF16)
        return carry

    lax.fori_loop(0, BLOCKS // 2, scale, 0)

    def help_tile(u, carry):
        t = 3 - u
        acc = weighted(1, t)
        ob_out[t] = (acc / stat[1, t, 8:9]).astype(BF16)
        send(ob_out.at[t], ob_in.at[t], o_send.at[t], o_recv.at[t], {"seq": across})
        send(stat.at[1, t], os_in.at[t], o_send.at[4 + t], o_recv.at[4 + t], {"seq": across})
        return carry

    lax.fori_loop(0, 4, help_tile, 0)

    def own_tile(u, carry):
        t = 3 - u
        acc = weighted(0, t)
        landed(ob_in.at[t], o_recv.at[t])
        landed(os_in.at[t], o_recv.at[4 + t])
        m0, m1 = stat[0, t, 0:1], os_in[t, 0:1]
        top = jnp.maximum(m0, m1)
        w0 = jnp.exp2((m0 - top) * factor)
        w1 = os_in[t, 8:9] * jnp.exp2((m1 - top) * factor)
        total = stat[0, t, 8:9] * w0 + w1
        merged = (acc * w0 + ob_in[t].astype(F32) * w1) / total
        out_ref[pl.ds(pl.multiple_of(t * 256, 256), 256), :] = merged.T.astype(BF16)
        return carry

    lax.fori_loop(0, 4, own_tile, 0)

    landed(rs.at[pl.ds(0, 63)], a_send.at[0])
    landed(kb.at[0, pl.ds(0, 63)], a_send.at[1])
    landed(rg.at[pl.ds(0, 63)], a_send.at[2])
    landed(qb.at[0], a_send.at[3])
    landed(qb.at[0, pl.ds(0, 63)], a_send.at[4])
    landed(hb.at[pl.ds(0, 63)], a_send.at[5])
    landed(inv_in.at[pl.ds(0, 63)], a_send.at[6])
    for n in range(7):
        landed(kb.at[0], k_send.at[n])
    for n in range(15):
        landed(vb.at[0], v_send.at[n])
    for t in range(4):
        landed(ob_in.at[t], o_send.at[t])
        landed(os_in.at[t], o_send.at[4 + t])
    for n in range(1, chan_count):
        landed(sq_in.at[0], o_send.at[8 + n])


def mega_call(sig, gate, taps, skip, q, k):
    return pl.pallas_call(
        mega_kernel,
        out_shape=(
            jax.ShapeDtypeStruct((ROWS, BLOCKS * CH), BF16),
            jax.ShapeDtypeStruct((BLOCKS * QR, HD), BF16),
        ),
        in_specs=[VMEM] * 6,
        out_specs=(VMEM, VMEM),
        scratch_shapes=[
            pltpu.VMEM((BLOCKS, CH, ROWS), BF16),
            pltpu.VMEM((BLOCKS, CH, ROWS), BF16),
            pltpu.VMEM((BLOCKS, CH, ROWS), BF16),
            pltpu.VMEM((BLOCKS, CH, ROWS), BF16),
            pltpu.VMEM((2, BLOCKS, QR, HD), BF16),
            pltpu.VMEM((8, BLOCKS, QR, HD), BF16),
            pltpu.VMEM((2, BLOCKS, CH, LANE), BF16),
            pltpu.VMEM((BLOCKS, 2, CH, LANE), BF16),
            pltpu.VMEM((SETS, BLOCKS, CH, LANE), BF16),
            pltpu.VMEM((1, ROWS), F32),
            pltpu.VMEM((4, 1, ROWS), F32),
            pltpu.VMEM((1, ROWS), F32),
            pltpu.VMEM((BLOCKS, 1, ROWS), F32),
            pltpu.VMEM((BLOCKS * ROWS, ROWS), BF16),
            pltpu.VMEM((576, ROWS), F32),
            pltpu.VMEM((512, 2048), BF16),
            pltpu.VMEM((512, ROWS), F32),
            pltpu.VMEM((BLOCKS // 2, 256, 256), F32),
            pltpu.VMEM((160, 256, 256), BF16),
            pltpu.VMEM((BLOCKS // 2, HD, 256), BF16),
            pltpu.VMEM((2, 4, 16, 256), F32),
            pltpu.VMEM((4, HD, 256), BF16),
            pltpu.VMEM((4, HD, 256), BF16),
            pltpu.VMEM((4, 16, 256), F32),
            pltpu.VMEM((4, 16, 256), F32),
            pltpu.SemaphoreType.DMA((7,)),
            pltpu.SemaphoreType.DMA((8,)),
            pltpu.SemaphoreType.DMA((7,)),
            pltpu.SemaphoreType.DMA((8,)),
            pltpu.SemaphoreType.DMA((15,)),
            pltpu.SemaphoreType.DMA((16,)),
            pltpu.SemaphoreType.DMA((12,)),
            pltpu.SemaphoreType.DMA((8,)),
        ],
        compiler_params=pltpu.CompilerParams(
            vmem_limit_bytes=62 * 2**20, collective_id=0, has_side_effects=True
        ),
        name="mega",
    )(sig, gate, taps, skip, q, k)


def shards(signal, gate_rows, skip_gain, filter_taps, queries, key_rows):
    me = lax.axis_index("seq")
    taps = lax.dynamic_slice_in_dim(filter_taps.T, me // SETS, 1, 0)
    taps = taps.reshape(LANE, LANE).astype(F32)
    skip = jnp.broadcast_to(lax.dynamic_slice_in_dim(skip_gain, me * CH, CH)[:, None], (CH, ROWS))
    mixed, attended = mega_call(signal, gate_rows, taps, skip, queries, key_rows)
    return mixed, attended[None]


def solution(mesh):
    in_specs = (
        P("seq", "chan"),
        P("seq", "chan"),
        P("chan"),
        P(None, "chan"),
        P("seq", "chan"),
        P("seq", "chan"),
    )
    out_specs = (P("seq", "chan"), P(("chan", "seq"), None, None))
    return jax.shard_map(shards, mesh=mesh, in_specs=in_specs, out_specs=out_specs, check_vma=False)
```

```python
import math

import jax
import jax.numpy as jnp
from jax import lax
from jax.experimental import pallas as pl
from jax.experimental.pallas import tpu as pltpu
from jax.sharding import PartitionSpec as P

ROWS = 256
BLOCKS = 64
HD = 128
SETS = 16
QR = 16
CH = 8
LANE = 128
F32 = jnp.float32
BF16 = jnp.bfloat16
MESH = pl.DeviceIdType.MESH
VMEM = pl.BlockSpec(memory_space=pltpu.VMEM)


def fill_toeplitz(taps_ref, gg_ref):
    row = lax.broadcasted_iota(jnp.int32, (LANE, LANE), 0)
    lane = lax.broadcasted_iota(jnp.int32, (LANE, LANE), 1)
    mask = lane >= row

    def rotated(chunk):
        line = jnp.broadcast_to(taps_ref[pl.ds(chunk, 1), :], (LANE, LANE))
        return pltpu.roll(line, 0, 1, stride=1, stride_axis=0)

    def body(d, carry):
        before, tile_before = carry
        first = rotated(2 * d)
        tile_a = jnp.where(mask, first, before).astype(BF16)
        second = rotated(2 * d + 1)
        tile_b = jnp.where(mask, second, first).astype(BF16)
        top = pl.ds(pl.multiple_of(d * 256, 256), LANE)
        low = pl.ds(pl.multiple_of(d * 256 + LANE, LANE), LANE)
        gg_ref[top, :LANE] = tile_a
        gg_ref[top, LANE:] = tile_b
        gg_ref[low, :LANE] = tile_before
        gg_ref[low, LANE:] = tile_a
        return second, tile_b

    lax.fori_loop(
        0, BLOCKS, body, (jnp.zeros((LANE, LANE), F32), jnp.zeros((LANE, LANE), BF16))
    )


def landed(ref, sem):
    pltpu.make_async_copy(ref, ref, sem).wait()


def fold_rows(x, op):
    return op(x.reshape(x.shape[0] // 8, 8, x.shape[1]), axis=0)


def tile_base(slot, t):
    return slot * 80 + 4 * t * (t + 1)


def mega_kernel(
    sig_ref, gate_ref, taps_ref, skip_ref, q_ref, k_ref,
    mixed_ref, out_ref,
    st_s, st_g, rs, rg, qb, kb, cmh, hb, vb, sq_out, sq_in, inv_out, inv_in,
    gg, xf, xx, acc_ref, s_ref, p_ref, vt_ref, stat, ob_out, ob_in, os_out, os_in,
    a_send, a_recv, k_send, k_recv, v_send, v_recv, o_send, o_recv,
):
    seq_count = lax.axis_size("seq")
    chan_count = lax.axis_size("chan")
    me = lax.axis_index("seq")
    my_chan = lax.axis_index("chan")
    core = me % 2
    y = (me // 2) % 4
    row0 = (me // 8) * 8
    zr = (me // 8) % 2
    my_set = me % SETS
    my_slot = me % 8
    other_core = me + 1 - 2 * core
    across = me + 8 - 16 * zr
    row1 = row0 + 8 - 16 * zr
    factor = (1.0 / math.sqrt(HD)) * math.log2(math.e)

    def send(src, dst, s_sem, r_sem, where):
        pltpu.make_async_remote_copy(
            src_ref=src, dst_ref=dst, send_sem=s_sem, recv_sem=r_sem,
            device_id=where, device_id_type=MESH,
        ).start()

    def others(body):
        def step(n, carry):
            body((me + n) % seq_count)
            return carry

        lax.fori_loop(1, seq_count, step, 0)

    def piece(ref, d):
        rows = pl.ds(pl.multiple_of((d % SETS) * QR, QR), QR)
        return ref.at[rows, pl.ds(pl.multiple_of((d // SETS) * HD, HD), HD)]

    st_s[...] = sig_ref[...].astype(F32).T.reshape(BLOCKS, CH, ROWS).astype(BF16)
    st_g[...] = gate_ref[...].astype(F32).T.reshape(BLOCKS, CH, ROWS).astype(BF16)

    barrier = pltpu.get_barrier_semaphore()
    others(
        lambda d: pl.semaphore_signal(
            barrier, inc=1, device_id={"seq": d}, device_id_type=MESH
        )
    )
    for n in range(1, chan_count):
        pl.semaphore_signal(
            barrier, inc=1, device_id={"chan": (my_chan + n) % chan_count}, device_id_type=MESH
        )
    pl.semaphore_wait(barrier, seq_count + chan_count - 2)

    others(lambda d: send(st_s.at[d], rs.at[me], a_send.at[0], a_recv.at[0], {"seq": d}))
    others(
        lambda d: send(
            piece(k_ref, d), kb.at[d % 8, me], a_send.at[1], a_recv.at[1], {"seq": d}
        )
    )
    others(lambda d: send(st_g.at[d], rg.at[me], a_send.at[2], a_recv.at[2], {"seq": d}))

    others(
        lambda d: send(
            piece(q_ref, d), qb.at[0, me], a_send.at[4], a_recv.at[4], {"seq": d}
        )
    )
    rs[me] = st_s[me]
    rg[me] = st_g[me]
    kb[my_slot, me] = piece(k_ref, me)[...]
    qb[0, me] = piece(q_ref, me)[...]

    fill_toeplitz(taps_ref, gg)
    xf[:64, :] = jnp.zeros((64, ROWS), F32)
    landed(rs.at[pl.ds(0, 63)], a_recv.at[0])
    xf[64:, :] = rs[...].astype(F32).reshape(BLOCKS * CH, ROWS)
    for e in range(8):
        xx[:, e * ROWS : (e + 1) * ROWS] = xf[64 - 8 * e : 576 - 8 * e, :].astype(BF16)
    acc_ref[...] = jnp.dot(xx[...], gg[:2048, :], preferred_element_type=F32)
    for g in range(1, 8):
        acc_ref[64 * g :, :] += jnp.dot(
            xx[: 512 - 64 * g, :],
            gg[2048 * g : 2048 * (g + 1), :],
            preferred_element_type=F32,
        )

    landed(kb.at[0, pl.ds(0, 63)], a_recv.at[1])
    row_mates = [row0 + ((y + n) % 4) * 2 + core for n in range(4)]
    far_mates = [row1 + ((y + n) % 4) * 2 + core for n in range(4)]
    for n in (1, 3, 2):
        send(
            kb.at[my_slot], kb.at[my_slot], k_send.at[n], k_recv.at[my_slot],
            {"seq": row_mates[n]},
        )
    send(kb.at[my_slot], kb.at[my_slot], k_send.at[0], k_recv.at[my_slot], {"seq": other_core})

    landed(rg.at[pl.ds(0, 63)], a_recv.at[2])
    conv = acc_ref[...].reshape(BLOCKS, CH, ROWS)
    lane = lax.broadcasted_iota(jnp.int32, (CH, BLOCKS * CH), 1)
    row = lax.broadcasted_iota(jnp.int32, (CH, BLOCKS * CH), 0)
    gains = jnp.broadcast_to(skip_ref[...], (CH, BLOCKS * CH))
    gains = jnp.sum(jnp.where(lane == me * CH + row, gains, 0.0), axis=1, keepdims=True)
    gains = jnp.broadcast_to(gains, (CH, ROWS))
    mixed = rg[...].astype(F32) * (conv + gains[None] * rs[...].astype(F32))
    mixed = mixed.astype(BF16)
    cmh[0] = mixed[:, :, :LANE]
    cmh[1] = mixed[:, :, LANE:]
    others(lambda d: send(cmh.at[:, d], hb.at[me], a_send.at[5], a_recv.at[5], {"seq": d}))
    hb[me] = cmh[:, me]
    send(cmh.at[1 - zr], vb.at[my_set], v_send.at[4], v_recv.at[my_set], {"seq": across})
    vb[my_set] = cmh[zr]
    for n in range(4):
        where = other_core if n == 0 else row_mates[n]
        send(cmh.at[zr], vb.at[my_set], v_send.at[n], v_recv.at[my_set], {"seq": where})

    for n in (1, 3, 2):
        slot = row_mates[n] % 8
        landed(kb.at[slot], k_recv.at[slot])
        send(kb.at[slot], kb.at[slot], k_send.at[3 + n], k_recv.at[slot], {"seq": other_core})
    for n in range(4):
        slot = row_mates[n] % 8 + 1 - 2 * core
        landed(kb.at[slot], k_recv.at[slot])

    def scores(slot, first, last):
        bq = (my_set + 8 * slot) % SETS

        def tile(t, carry):
            base = tile_base(slot, t)
            q = qb[slot, pl.ds(t * SETS, SETS)].reshape(256, HD)
            qt = q.astype(F32).T.astype(BF16)
            qt_hi = qt[:, LANE:]

            def keys(p):
                return jnp.concatenate(
                    [kb[:, 2 * p].reshape(LANE, HD), kb[:, 2 * p + 1].reshape(LANE, HD)], axis=0
                )

            def plain(u, m):
                for p in (2 * u, 2 * u + 1):
                    s = jnp.dot(keys(p), qt, preferred_element_type=F32)
                    s_ref[p] = s
                    m = jnp.maximum(m, fold_rows(s, jnp.max))
                return m

            def masked(p, width, lane0):
                s = jnp.dot(
                    keys(p), qt if width == 256 else qt_hi, preferred_element_type=F32
                )
                lanes = lax.broadcasted_iota(jnp.int32, (256, width), 1) + lane0
                rows = lax.broadcasted_iota(jnp.int32, (256, width), 0)
                q_pos = (lanes // QR) * ROWS + lanes % QR
                k_pos = (rows // LANE) * ROWS + rows % LANE
                shift = 16 * t * ROWS + bq * QR - 2 * p * ROWS - zr * LANE
                return jnp.where(k_pos - q_pos <= shift, s, -1e30)

            def diag(u, m):
                p = 8 * t + u
                s = masked(p, 256, 0)
                s_ref[p] = s
                return jnp.maximum(m, fold_rows(s, jnp.max))

            def diag_hi(u, m):
                p = 8 * t + 4 + u
                s = masked(p, LANE, LANE)
                s_ref[p, :, LANE:] = s
                return jnp.maximum(m, fold_rows(s, jnp.max))

            m = jnp.full((8, 256), -1e30, F32)
            m = lax.fori_loop(0, 4 * t, plain, m)
            m = lax.fori_loop(0, 4, diag, m, unroll=2)
            m_hi = lax.fori_loop(0, 4, diag_hi, m[:, LANE:], unroll=2)
            m = jnp.concatenate([m[:, :LANE], m_hi], axis=1)
            peak = jnp.max(m, axis=0, keepdims=True)

            def weigh(p, total):
                w = jnp.exp2((s_ref[p] - peak) * factor)
                p_ref[base + p] = w.astype(BF16)
                return total + fold_rows(w, jnp.sum)

            def weigh_two(u, total):
                return weigh(2 * u + 1, weigh(2 * u, total))

            def weigh_hi(u, total):
                p = 8 * t + 4 + u
                w = jnp.exp2((s_ref[p, :, LANE:] - peak[:, LANE:]) * factor)
                p_ref[base + p, :, LANE:] = w.astype(BF16)
                return total + fold_rows(w, jnp.sum)

            total = lax.fori_loop(0, 4 * t + 2, weigh_two, jnp.zeros((8, 256), F32))
            total_hi = lax.fori_loop(0, 4, weigh_hi, total[:, LANE:], unroll=2)
            total = jnp.concatenate([total[:, :LANE], total_hi], axis=1)
            stat[slot, t, :8] = jnp.broadcast_to(peak, (8, 256))
            stat[slot, t, 8:] = jnp.broadcast_to(
                jnp.sum(total, axis=0, keepdims=True), (8, 256)
            )
            return carry

        lax.fori_loop(first, last, tile, 0)

    def weighted(slot, t):
        base = tile_base(slot, t)

        def both(u, acc):
            for p in (2 * u, 2 * u + 1):
                acc = acc + jnp.dot(vt_ref[p], p_ref[base + p], preferred_element_type=F32)
            return acc

        def high(u, acc):
            p = 8 * t + 4 + u
            return acc + jnp.dot(
                vt_ref[p], p_ref[base + p, :, LANE:], preferred_element_type=F32
            )

        acc = lax.fori_loop(0, 4 * t + 2, both, jnp.zeros((HD, 256), F32))
        acc_hi = lax.fori_loop(0, 4, high, acc[:, LANE:], unroll=2)
        return jnp.concatenate([acc[:, :LANE], acc_hi], axis=1)

    def pass_values(n):
        slot = (row_mates[n] if n < 4 else far_mates[n - 4]) % SETS
        landed(vb.at[slot], v_recv.at[slot])
        send(vb.at[slot], vb.at[slot], v_send.at[8 + n - n // 4], v_recv.at[slot], {"seq": other_core})

    landed(qb.at[0, pl.ds(0, 63)], a_recv.at[4])
    send(qb.at[0], qb.at[1], a_send.at[3], a_recv.at[3], {"seq": across})
    scores(0, 0, 3)

    landed(hb.at[pl.ds(0, 63)], a_recv.at[5])
    for half in range(2):
        lanes = slice(half * LANE, (half + 1) * LANE)
        wide = hb[:, half].astype(F32).reshape(BLOCKS * CH, LANE)
        sq_out[:, lanes] = jnp.sum(fold_rows(wide * wide, jnp.sum), axis=0, keepdims=True)
    sq_in[my_chan] = sq_out[...]
    for n in range(1, chan_count):
        send(
            sq_out, sq_in.at[my_chan], o_send.at[8 + n], a_recv.at[6],
            {"chan": (my_chan + n) % chan_count},
        )
    for half in range(2):
        wide = hb[:, half].astype(F32).reshape(BLOCKS * CH, LANE)
        mixed_ref[half * LANE : (half + 1) * LANE, :] = wide.T.astype(BF16)

    far = across % SETS
    landed(vb.at[far], v_recv.at[far])
    for n in (1, 3, 2):
        send(vb.at[far], vb.at[far], v_send.at[4 + n], v_recv.at[far], {"seq": row_mates[n]})
    send(vb.at[far], vb.at[far], v_send.at[8], v_recv.at[far], {"seq": other_core})
    scores(0, 3, 4)

    if chan_count > 1:
        landed(sq_in.at[pl.ds(0, chan_count - 1)], a_recv.at[6])
    whole = sq_in[0]
    for n in range(1, chan_count):
        whole = whole + sq_in[n]
    inv_out[...] = lax.rsqrt(whole / (BLOCKS * CH * chan_count) + 1e-06)
    others(lambda d: send(inv_out, inv_in.at[me], a_send.at[6], a_recv.at[7], {"seq": d}))
    inv_in[me] = inv_out[...]

    for n in (1, 3, 2):
        pass_values(n)
    landed(qb.at[1], a_recv.at[3])
    scores(1, 0, 3)
    for n in (5, 7, 6):
        pass_values(n)
    scores(1, 3, 4)

    for n in range(8):
        slot = (row_mates[n] if n < 4 else far_mates[n - 4]) % SETS + 1 - 2 * core
        landed(vb.at[slot], v_recv.at[slot])
    landed(inv_in.at[pl.ds(0, 63)], a_recv.at[7])

    def scale(p, carry):
        for u in range(2):
            v = vb[:, 2 * p + u].astype(F32).reshape(HD, LANE)
            inv = inv_in[2 * p + u, :, pl.ds(pl.multiple_of(zr * LANE, LANE), LANE)]
            vt_ref[p, :, u * LANE : (u + 1) * LANE] = (v * inv).astype(BF16)
        return carry

    lax.fori_loop(0, BLOCKS // 2, scale, 0)

    def help_tile(u, carry):
        t = 3 - u
        acc = weighted(1, t)
        ob_out[t] = (acc / stat[1, t, 8:9]).astype(BF16)
        send(ob_out.at[t], ob_in.at[t], o_send.at[t], o_recv.at[t], {"seq": across})
        send(stat.at[1, t], os_in.at[t], o_send.at[4 + t], o_recv.at[4 + t], {"seq": across})
        return carry

    lax.fori_loop(0, 4, help_tile, 0)

    def own_tile(u, carry):
        t = 3 - u
        acc = weighted(0, t)
        landed(ob_in.at[t], o_recv.at[t])
        landed(os_in.at[t], o_recv.at[4 + t])
        m0, m1 = stat[0, t, 0:1], os_in[t, 0:1]
        top = jnp.maximum(m0, m1)
        w0 = jnp.exp2((m0 - top) * factor)
        w1 = os_in[t, 8:9] * jnp.exp2((m1 - top) * factor)
        total = stat[0, t, 8:9] * w0 + w1
        merged = (acc * w0 + ob_in[t].astype(F32) * w1) / total
        out_ref[pl.ds(pl.multiple_of(t * 256, 256), 256), :] = merged.T.astype(BF16)
        return carry

    lax.fori_loop(0, 4, own_tile, 0)

    landed(rs.at[pl.ds(0, 63)], a_send.at[0])
    landed(kb.at[0, pl.ds(0, 63)], a_send.at[1])
    landed(rg.at[pl.ds(0, 63)], a_send.at[2])
    landed(qb.at[0], a_send.at[3])
    landed(qb.at[0, pl.ds(0, 63)], a_send.at[4])
    landed(hb.at[pl.ds(0, 63)], a_send.at[5])
    landed(inv_in.at[pl.ds(0, 63)], a_send.at[6])
    for n in range(7):
        landed(kb.at[0], k_send.at[n])
    for n in range(15):
        landed(vb.at[0], v_send.at[n])
    for t in range(4):
        landed(ob_in.at[t], o_send.at[t])
        landed(os_in.at[t], o_send.at[4 + t])
    for n in range(1, chan_count):
        landed(sq_in.at[0], o_send.at[8 + n])


def mega_call(sig, gate, taps, skip, q, k):
    return pl.pallas_call(
        mega_kernel,
        out_shape=(
            jax.ShapeDtypeStruct((ROWS, BLOCKS * CH), BF16),
            jax.ShapeDtypeStruct((BLOCKS * QR, HD), BF16),
        ),
        in_specs=[VMEM] * 6,
        out_specs=(VMEM, VMEM),
        scratch_shapes=[
            pltpu.VMEM((BLOCKS, CH, ROWS), BF16),
            pltpu.VMEM((BLOCKS, CH, ROWS), BF16),
            pltpu.VMEM((BLOCKS, CH, ROWS), BF16),
            pltpu.VMEM((BLOCKS, CH, ROWS), BF16),
            pltpu.VMEM((2, BLOCKS, QR, HD), BF16),
            pltpu.VMEM((8, BLOCKS, QR, HD), BF16),
            pltpu.VMEM((2, BLOCKS, CH, LANE), BF16),
            pltpu.VMEM((BLOCKS, 2, CH, LANE), BF16),
            pltpu.VMEM((SETS, BLOCKS, CH, LANE), BF16),
            pltpu.VMEM((1, ROWS), F32),
            pltpu.VMEM((4, 1, ROWS), F32),
            pltpu.VMEM((1, ROWS), F32),
            pltpu.VMEM((BLOCKS, 1, ROWS), F32),
            pltpu.VMEM((BLOCKS * ROWS, ROWS), BF16),
            pltpu.VMEM((576, ROWS), F32),
            pltpu.VMEM((512, 2048), BF16),
            pltpu.VMEM((512, ROWS), F32),
            pltpu.VMEM((BLOCKS // 2, 256, 256), F32),
            pltpu.VMEM((160, 256, 256), BF16),
            pltpu.VMEM((BLOCKS // 2, HD, 256), BF16),
            pltpu.VMEM((2, 4, 16, 256), F32),
            pltpu.VMEM((4, HD, 256), BF16),
            pltpu.VMEM((4, HD, 256), BF16),
            pltpu.VMEM((4, 16, 256), F32),
            pltpu.VMEM((4, 16, 256), F32),
            pltpu.SemaphoreType.DMA((7,)),
            pltpu.SemaphoreType.DMA((8,)),
            pltpu.SemaphoreType.DMA((7,)),
            pltpu.SemaphoreType.DMA((8,)),
            pltpu.SemaphoreType.DMA((15,)),
            pltpu.SemaphoreType.DMA((16,)),
            pltpu.SemaphoreType.DMA((12,)),
            pltpu.SemaphoreType.DMA((8,)),
        ],
        compiler_params=pltpu.CompilerParams(
            vmem_limit_bytes=62 * 2**20, collective_id=0, has_side_effects=True
        ),
        name="mega",
    )(sig, gate, taps, skip, q, k)


def shards(signal, gate_rows, skip_gain, filter_taps, queries, key_rows):
    me = lax.axis_index("seq")
    taps = lax.dynamic_slice_in_dim(filter_taps.T, me // SETS, 1, 0)
    taps = taps.reshape(LANE, LANE).astype(F32)
    skip = skip_gain.reshape(1, BLOCKS * CH)
    mixed, attended = mega_call(signal, gate_rows, taps, skip, queries, key_rows)
    return mixed, attended[None]


def solution(mesh):
    in_specs = (
        P("seq", "chan"),
        P("seq", "chan"),
        P("chan"),
        P(None, "chan"),
        P("seq", "chan"),
        P("seq", "chan"),
    )
    out_specs = (P("seq", "chan"), P(("chan", "seq"), None, None))
    return jax.shard_map(shards, mesh=mesh, in_specs=in_specs, out_specs=out_specs, check_vma=False)
```
